32 devices in a mesh: row: 8 (over z, x), col: 4 (over y, core).
Axes of the slice: x: 2, y: 2, z: 4, core: 2. Of those that a mesh axis runs over, the one named last changes fastest.
Arguments:
- inputs: float32 [2048, 960], P('row', 'col'), may hold values from -8 to 8
- query_one: bfloat16 [960, 960], P('row', 'col'), may hold values from -1 to 1
- key_one: bfloat16 [960, 320], P('row', 'col'), may hold values from -1 to 1
- value_one: bfloat16 [960, 320], P('row', 'col'), may hold values from -1 to 1
- output_one: bfloat16 [960, 960], P('row', 'col'), may hold values from -1.5 to 1.5
- gate_one: bfloat16 [960, 2560], P('row', 'col'), may hold values from -0.1875 to 0.1875
- up_one: bfloat16 [960, 2560], P('row', 'col'), may hold values from -0.1875 to 0.1875
- down_one: bfloat16 [2560, 960], P('row', 'col'), may hold values from -0.125 to 0.125
- attn_gain_one: float32 [960], P('col'), may hold values from 0.5 to 1.5
- ffn_gain_one: float32 [960], P('col'), may hold values from 0.5 to 1.5
- query_two: bfloat16 [960, 960], P('row', 'col'), may hold values from -1 to 1
- key_two: bfloat16 [960, 320], P('row', 'col'), may hold values from -1 to 1
- value_two: bfloat16 [960, 320], P('row', 'col'), may hold values from -1 to 1
- output_two: bfloat16 [960, 960], P('row', 'col'), may hold values from -1.5 to 1.5
- gate_two: bfloat16 [960, 2560], P('row', 'col'), may hold values from -0.1875 to 0.1875
- up_two: bfloat16 [960, 2560], P('row', 'col'), may hold values from -0.1875 to 0.1875
- down_two: bfloat16 [2560, 960], P('row', 'col'), may hold values from -0.125 to 0.125
- attn_gain_two: float32 [960], P('col'), may hold values from 0.5 to 1.5
- ffn_gain_two: float32 [960], P('col'), may hold values from 0.5 to 1.5
- cotangent: float32 [2048, 960], P('row', 'col'), may hold values from -6 to 6
Outputs:
- result: float32 [2048, 960], P('row', 'col')
- inputs_grad: float32 [2048, 960], P('row', 'col')
- query_one_grad: float32 [960, 960], P('row', 'col')
- key_one_grad: float32 [960, 320], P('row', 'col')
- value_one_grad: float32 [960, 320], P('row', 'col')
- output_one_grad: float32 [960, 960], P('row', 'col')
- gate_one_grad: float32 [960, 2560], P('row', 'col')
- up_one_grad: float32 [960, 2560], P('row', 'col')
- down_one_grad: float32 [2560, 960], P('row', 'col')
- attn_gain_one_grad: float32 [960], P('col')
- ffn_gain_one_grad: float32 [960], P('col')
- query_two_grad: float32 [960, 960], P('row', 'col')
- key_two_grad: float32 [960, 320], P('row', 'col')
- value_two_grad: float32 [960, 320], P('row', 'col')
- output_two_grad: float32 [960, 960], P('row', 'col')
- gate_two_grad: float32 [960, 2560], P('row', 'col')
- up_two_grad: float32 [960, 2560], P('row', 'col')
- down_two_grad: float32 [2560, 960], P('row', 'col')
- attn_gain_two_grad: float32 [960], P('col')
- ffn_gain_two_grad: float32 [960], P('col')
The draws below stay inside these ranges and needn't reach their ends.
All inputs are finite; a program needn't handle non-finite values.
Results may differ from the reference program's by a relative error of at most 0.028.
The reference program's roundings to bfloat16 on the way (of `normed_one`, `attended`, `normed_two`, `hidden`, `grad_attended` and `grad_scores`) count: a program that leaves them out, or rounds other values in their place, can miss the bound.
Values may be sent and summed in bfloat16 or wider, within the bound.
A program may use at most 128 MiB of HBM per device.

```python
import math
import jax
import jax.numpy as jnp
from jax import lax

D = 960
HEADS = 15
KV_HEADS = 5
HEAD_DIM = 64
FF = 2560
SEQ_LEN = 128
QW = 960
KW = 320
ROWS = 256
TOKENS = 2048


def drawn_weight(key, tag, columns):
    values = jax.random.truncated_normal(jax.random.fold_in(key, tag), -6.0, 6.0, (D, columns), jnp.float32)
    return values / jnp.sqrt(jnp.float32(D))


def spiked_weight(key, tag, heads):
    values = drawn_weight(key, tag, heads * HEAD_DIM)
    return jnp.clip(values, -1.0, 1.0)


def damped_weight(key, tag):
    values = drawn_weight(key, tag, KW)
    return jnp.clip(values, -1.0, 1.0)


def draw_inputs(key, part):
    values = jax.random.truncated_normal(jax.random.fold_in(key, 10), -6.0, 6.0, (TOKENS, D), jnp.float32)
    return jnp.clip(values, -8.0, 8.0)


def draw_query_one(key, part):
    return spiked_weight(key, 110, HEADS).astype(jnp.bfloat16)


def draw_key_one(key, part):
    return spiked_weight(key, 120, KV_HEADS).astype(jnp.bfloat16)


def draw_value_one(key, part):
    return damped_weight(key, 130).astype(jnp.bfloat16)


def draw_query_two(key, part):
    return spiked_weight(key, 210, HEADS).astype(jnp.bfloat16)


def draw_key_two(key, part):
    return spiked_weight(key, 220, KV_HEADS).astype(jnp.bfloat16)


def draw_value_two(key, part):
    return damped_weight(key, 230).astype(jnp.bfloat16)


def block_levels(stream_key, shape, shards, low, top_value):
    level = 1.0
    for axis_at, parts in shards:
        steps = jax.random.uniform(jax.random.fold_in(jax.random.fold_in(stream_key, 6), axis_at), (parts,), jnp.float32, low / len(shards), top_value / len(shards))
        level = level * jnp.repeat(jnp.exp(steps), shape[axis_at] // parts).reshape((-1,) + (1,) * (len(shape) - 1 - axis_at))
    return level


def centred(own_key, shape, spread, reach, split=(), held_as=jnp.bfloat16):
    entries = spread * jax.random.normal(own_key, shape, jnp.float32)
    if split:
        entries = entries * block_levels(own_key, shape, split, -0.22, 0.18)
    return jnp.clip(entries, -reach, reach).astype(held_as)


def setup_inputs(seed: int = 0) -> dict:
    arg_keys = jax.random.split(jax.random.key(seed), 21)
    return {
        "inputs": draw_inputs(jax.random.fold_in(arg_keys[20], 71), 0),
        "query_one": draw_query_one(jax.random.fold_in(arg_keys[20], 71), 0),
        "key_one": draw_key_one(jax.random.fold_in(arg_keys[20], 71), 0),
        "value_one": draw_value_one(jax.random.fold_in(arg_keys[20], 71), 0),
        "output_one": centred(arg_keys[4], (QW, D), (max(QW // 64, 4)) ** -0.5, 1.5, ((0, 8), (1, 4))),
        "gate_one": centred(arg_keys[5], (D, FF), D ** -0.5, 0.1875, ((0, 8), (1, 4))),
        "up_one": centred(arg_keys[6], (D, FF), D ** -0.5, 0.1875, ((0, 8), (1, 4))),
        "down_one": centred(arg_keys[7], (FF, D), FF ** -0.5, 0.125, ((0, 8), (1, 4))),
        "attn_gain_one": jnp.clip(1.0 + 0.1 * jax.random.normal(arg_keys[8], (D,), jnp.float32), 0.5, 1.5),
        "ffn_gain_one": jnp.clip(1.0 + 0.1 * jax.random.normal(arg_keys[9], (D,), jnp.float32), 0.5, 1.5),
        "query_two": draw_query_two(jax.random.fold_in(arg_keys[20], 71), 0),
        "key_two": draw_key_two(jax.random.fold_in(arg_keys[20], 71), 0),
        "value_two": draw_value_two(jax.random.fold_in(arg_keys[20], 71), 0),
        "output_two": centred(arg_keys[13], (QW, D), (max(QW // 64, 4)) ** -0.5, 1.5, ((0, 8), (1, 4))),
        "gate_two": centred(arg_keys[14], (D, FF), D ** -0.5, 0.1875, ((0, 8), (1, 4))),
        "up_two": centred(arg_keys[15], (D, FF), D ** -0.5, 0.1875, ((0, 8), (1, 4))),
        "down_two": centred(arg_keys[16], (FF, D), FF ** -0.5, 0.125, ((0, 8), (1, 4))),
        "attn_gain_two": jnp.clip(1.0 + 0.1 * jax.random.normal(arg_keys[17], (D,), jnp.float32), 0.5, 1.5),
        "ffn_gain_two": jnp.clip(1.0 + 0.1 * jax.random.normal(arg_keys[18], (D,), jnp.float32), 0.5, 1.5),
        "cotangent": centred(arg_keys[19], (TOKENS, D), 1.0, 6.0, ((0, 8), (1, 4)), jnp.float32),
    }


EPS = 1e-05
ROPE_BASE = 100000.0
NEG_FILL = -1e+30

def rope_tables(length, depth):
    half = depth // 2
    frequency = ROPE_BASE ** (-(jnp.arange(half, dtype=jnp.float32) * 2.0) / depth)
    angles = jnp.arange(length, dtype=jnp.float32)[:, None] * frequency[None, :]
    return (jnp.cos(angles), jnp.sin(angles))

def rotate(values, cosines, sines):
    half = values.shape[-1] // 2
    first = values[..., :half]
    second = values[..., half:]
    cosine = cosines[:, None, :]
    sine = sines[:, None, :]
    return jnp.concatenate([first * cosine - second * sine, second * cosine + first * sine], axis=-1)

def unrotate(values, cosines, sines):
    half = values.shape[-1] // 2
    first = values[..., :half]
    second = values[..., half:]
    cosine = cosines[:, None, :]
    sine = sines[:, None, :]
    return jnp.concatenate([first * cosine + second * sine, second * cosine - first * sine], axis=-1)

def rounded_copy(values):
    return lax.optimization_barrier(values.astype(jnp.bfloat16)).astype(jnp.float32)

def causal_scores(query, keys):
    scale = 1.0 / math.sqrt(HEAD_DIM)
    scores = jnp.einsum('qhd,khd->hqk', query.astype(jnp.float32), keys.astype(jnp.float32)) * scale
    length = query.shape[0]
    allowed = jnp.arange(length)[None, :] <= jnp.arange(length)[:, None]
    return jnp.where(allowed[None], scores, NEG_FILL)

def attend(query, keys, values):
    scores = causal_scores(query, keys)
    top = lax.optimization_barrier(jnp.max(scores, axis=-1, keepdims=True))
    log_total = top + jnp.log(lax.optimization_barrier(jnp.sum(jnp.exp(scores - top), axis=-1, keepdims=True)))
    shares = rounded_copy(jnp.exp(scores - log_total))
    output = jnp.einsum('hqk,khd->qhd', shares, values.astype(jnp.float32)).astype(jnp.bfloat16)
    return (output, log_total[..., 0])

def attend_back(query, keys, values, log_total, grad_output):
    scale = 1.0 / math.sqrt(HEAD_DIM)
    scores = causal_scores(query, keys)
    shares = jnp.exp(scores - log_total[..., None])
    grad_wide = grad_output.astype(jnp.float32)
    grad_values = jnp.einsum('hqk,qhd->khd', rounded_copy(shares), grad_wide)
    grad_shares = jnp.einsum('qhd,khd->hqk', grad_wide, values.astype(jnp.float32))
    inner = lax.optimization_barrier(jnp.sum(shares * grad_shares, axis=-1, keepdims=True))
    grad_scores = rounded_copy(shares * (grad_shares - inner) * scale)
    grad_query = jnp.einsum('hqk,khd->qhd', grad_scores, keys.astype(jnp.float32))
    grad_keys = jnp.einsum('hqk,qhd->khd', grad_scores, query.astype(jnp.float32))
    return (grad_query, grad_keys, grad_values)

def attend_sequence(pieces):
    query, keys, values = pieces
    group = HEADS // KV_HEADS
    return attend(query, jnp.repeat(keys, group, axis=1), jnp.repeat(values, group, axis=1))

def attend_back_sequence(pieces):
    query, keys, values, log_total, grad_output = pieces
    group = HEADS // KV_HEADS
    length = query.shape[0]
    grad_query, grad_keys, grad_values = attend_back(query, jnp.repeat(keys, group, axis=1), jnp.repeat(values, group, axis=1), log_total, grad_output)
    grad_keys = grad_keys.reshape(length, KV_HEADS, group, HEAD_DIM).sum(axis=2)
    grad_values = grad_values.reshape(length, KV_HEADS, group, HEAD_DIM).sum(axis=2)
    return (grad_query, grad_keys, grad_values)

def product(left, right):
    return jnp.dot(left, right, preferred_element_type=jnp.float32)

def norm_back(grad_normed, stream, scale, gain):
    grad_gain = lax.optimization_barrier(jnp.sum(grad_normed * stream * scale, axis=0))
    scaled = grad_normed * gain
    slope = lax.optimization_barrier(jnp.mean(scaled * stream, axis=1, keepdims=True))
    return (scale * scaled - stream * scale ** 3 * slope, grad_gain)

def layer_forward(stream, weights, gain_attn, gain_ffn):
    query_w, key_w, value_w, output_w, gate_w, up_w, down_w = weights
    cosines, sines = rope_tables(SEQ_LEN, HEAD_DIM)
    length = stream.shape[0]
    sequences = length // SEQ_LEN
    scale_one = lax.rsqrt(lax.optimization_barrier(jnp.mean(stream * stream, axis=1, keepdims=True)) + EPS)
    normed_one = (stream * scale_one * gain_attn).astype(jnp.bfloat16)
    query = product(normed_one, query_w).astype(jnp.bfloat16)
    keys = product(normed_one, key_w).astype(jnp.bfloat16)
    values = product(normed_one, value_w).astype(jnp.bfloat16)
    query_rot = rotate(query.reshape(sequences, SEQ_LEN, HEADS, HEAD_DIM).astype(jnp.float32), cosines, sines).astype(jnp.bfloat16)
    keys_rot = rotate(keys.reshape(sequences, SEQ_LEN, KV_HEADS, HEAD_DIM).astype(jnp.float32), cosines, sines).astype(jnp.bfloat16)
    values_four = values.reshape(sequences, SEQ_LEN, KV_HEADS, HEAD_DIM)
    attended, log_total = lax.map(attend_sequence, (query_rot, keys_rot, values_four))
    attended_flat = attended.reshape(length, HEADS * HEAD_DIM)
    middle = stream + product(attended_flat, output_w)
    scale_two = lax.rsqrt(lax.optimization_barrier(jnp.mean(middle * middle, axis=1, keepdims=True)) + EPS)
    normed_two = (middle * scale_two * gain_ffn).astype(jnp.bfloat16)
    gate = product(normed_two, gate_w)
    up = product(normed_two, up_w)
    hidden = (jax.nn.silu(gate) * up).astype(jnp.bfloat16)
    result = middle + product(hidden, down_w)
    saved = (scale_one, normed_one, query_rot, keys_rot, values_four, log_total, attended_flat, middle, scale_two, normed_two, gate, up, hidden)
    return (result, saved)

def layer_backward(stream, weights, gain_attn, gain_ffn, saved, grad_result):
    query_w, key_w, value_w, output_w, gate_w, up_w, down_w = weights
    scale_one, normed_one, query_rot, keys_rot, values_four, log_total, attended_flat, middle, scale_two, normed_two, gate, up, hidden = saved
    cosines, sines = rope_tables(SEQ_LEN, HEAD_DIM)
    length = stream.shape[0]
    sequences = length // SEQ_LEN
    grad_low = grad_result.astype(jnp.bfloat16)
    grad_down = product(hidden.T, grad_low)
    grad_hidden = product(grad_low, down_w.T)
    sigma = jax.nn.sigmoid(gate)
    grad_gate = (grad_hidden * up * sigma * (1.0 + gate * (1.0 - sigma))).astype(jnp.bfloat16)
    grad_up = (grad_hidden * jax.nn.silu(gate)).astype(jnp.bfloat16)
    grad_gate_w = product(normed_two.T, grad_gate)
    grad_up_w = product(normed_two.T, grad_up)
    grad_normed_two = product(grad_gate, gate_w.T) + product(grad_up, up_w.T)
    grad_middle, grad_gain_ffn = norm_back(grad_normed_two, middle, scale_two, gain_ffn)
    grad_middle = grad_middle + grad_result
    middle_low = grad_middle.astype(jnp.bfloat16)
    grad_output_w = product(attended_flat.T, middle_low)
    grad_attended = product(middle_low, output_w.T).astype(jnp.bfloat16).reshape(sequences, SEQ_LEN, HEADS, HEAD_DIM)
    grad_query_rot, grad_keys_rot, grad_values_four = lax.map(attend_back_sequence, (query_rot, keys_rot, values_four, log_total, grad_attended))
    grad_query = unrotate(grad_query_rot, cosines, sines).astype(jnp.bfloat16).reshape(length, HEADS * HEAD_DIM)
    grad_keys = unrotate(grad_keys_rot, cosines, sines).astype(jnp.bfloat16).reshape(length, KV_HEADS * HEAD_DIM)
    grad_values = grad_values_four.astype(jnp.bfloat16).reshape(length, KV_HEADS * HEAD_DIM)
    grad_query_w = product(normed_one.T, grad_query)
    grad_key_w = product(normed_one.T, grad_keys)
    grad_value_w = product(normed_one.T, grad_values)
    grad_normed_one = product(grad_query, query_w.T) + product(grad_keys, key_w.T) + product(grad_values, value_w.T)
    grad_stream, grad_gain_attn = norm_back(grad_normed_one, stream, scale_one, gain_attn)
    grad_stream = grad_stream + grad_middle
    grads = (grad_query_w, grad_key_w, grad_value_w, grad_output_w, grad_gate_w, grad_up_w, grad_down, grad_gain_attn, grad_gain_ffn)
    return (grad_stream, grads)

def reference(inputs, query_one, key_one, value_one, output_one, gate_one, up_one, down_one, attn_gain_one, ffn_gain_one, query_two, key_two, value_two, output_two, gate_two, up_two, down_two, attn_gain_two, ffn_gain_two, cotangent):
    first = (query_one, key_one, value_one, output_one, gate_one, up_one, down_one)
    second = (query_two, key_two, value_two, output_two, gate_two, up_two, down_two)
    blocks = TOKENS // ROWS

    def block_step(totals, pieces):
        input_block, cotangent_block = pieces
        between, saved_one = layer_forward(input_block, first, attn_gain_one, ffn_gain_one)
        result_block, saved_two = layer_forward(between, second, attn_gain_two, ffn_gain_two)
        grad_between, grads_two = layer_backward(between, second, attn_gain_two, ffn_gain_two, saved_two, cotangent_block)
        grad_block, grads_one = layer_backward(input_block, first, attn_gain_one, ffn_gain_one, saved_one, grad_between)
        updated = tuple((total + piece for total, piece in zip(totals, grads_one + grads_two)))
        return (updated, (result_block, grad_block))
    shapes = [weight.shape for weight in first] + [attn_gain_one.shape, ffn_gain_one.shape] + [weight.shape for weight in second] + [attn_gain_two.shape, ffn_gain_two.shape]
    start = tuple((jnp.zeros(shape, jnp.float32) for shape in shapes))
    totals, outputs = lax.scan(block_step, start, (inputs.reshape(blocks, ROWS, D), cotangent.reshape(blocks, ROWS, D)))
    grad_factor = jnp.float32(1.0 / math.sqrt(TOKENS))
    totals = tuple((total * grad_factor for total in totals))
    result = outputs[0].reshape(TOKENS, D)
    grad_inputs = outputs[1].reshape(TOKENS, D)
    return (result, grad_inputs, totals[0], totals[1], totals[2], totals[3], totals[4], totals[5], totals[6], totals[7], totals[8], totals[9], totals[10], totals[11], totals[12], totals[13], totals[14], totals[15], totals[16], totals[17])
```

```python
import functools
import math

import jax
import jax.numpy as jnp
from jax import lax
from jax.experimental import pallas as pl
from jax.experimental.pallas import tpu as pltpu
from jax.sharding import PartitionSpec as P

HEADS = 15
KV_HEADS = 5
HEAD_DIM = 64
SEQ_LEN = 128


EPS = 1e-05
ROPE_BASE = 100000.0
NEG_FILL = -1e30


def rope_tables(length, depth):
    half = depth // 2
    frequency = ROPE_BASE ** (-(jnp.arange(half, dtype=jnp.float32) * 2.0) / depth)
    angles = jnp.arange(length, dtype=jnp.float32)[:, None] * frequency[None, :]
    return (jnp.cos(angles), jnp.sin(angles))


def rotate(values, cosines, sines):
    half = values.shape[-1] // 2
    first = values[..., :half]
    second = values[..., half:]
    cosine = cosines[:, None, :]
    sine = sines[:, None, :]
    return jnp.concatenate(
        [first * cosine - second * sine, second * cosine + first * sine], axis=-1
    )


def unrotate(values, cosines, sines):
    half = values.shape[-1] // 2
    first = values[..., :half]
    second = values[..., half:]
    cosine = cosines[:, None, :]
    sine = sines[:, None, :]
    return jnp.concatenate(
        [first * cosine + second * sine, second * cosine - first * sine], axis=-1
    )


def product(left, right):
    return jnp.dot(left, right, preferred_element_type=jnp.float32)


def causal_scores(query, keys):
    scale = 1.0 / math.sqrt(query.shape[-1])
    scores = jnp.einsum("sqhd,skhd->shqk", query, keys, preferred_element_type=jnp.float32) * scale
    length = query.shape[1]
    allowed = jnp.arange(length)[None, :] <= jnp.arange(length)[:, None]
    return jnp.where(allowed[None, None], scores, NEG_FILL)


def attend(query, keys, values):
    scores = causal_scores(query, keys)
    top = jnp.max(scores, axis=-1, keepdims=True)
    log_total = top + jnp.log(jnp.sum(jnp.exp(scores - top), axis=-1, keepdims=True))
    shares = jnp.exp(scores - log_total).astype(jnp.bfloat16)
    output = jnp.einsum(
        "shqk,skhd->sqhd", shares, values, preferred_element_type=jnp.float32
    ).astype(jnp.bfloat16)
    return (output, log_total[..., 0])


def attend_back(query, keys, values, log_total, grad_output):
    scale = 1.0 / math.sqrt(query.shape[-1])
    scores = causal_scores(query, keys)
    shares = jnp.exp(scores - log_total[..., None])
    grad_values = jnp.einsum(
        "shqk,sqhd->skhd",
        shares.astype(jnp.bfloat16),
        grad_output,
        preferred_element_type=jnp.float32,
    )
    grad_shares = jnp.einsum(
        "sqhd,skhd->shqk", grad_output, values, preferred_element_type=jnp.float32
    )
    inner = jnp.sum(shares * grad_shares, axis=-1, keepdims=True)
    grad_scores = (shares * (grad_shares - inner) * scale).astype(jnp.bfloat16)
    grad_query = jnp.einsum(
        "shqk,skhd->sqhd", grad_scores, keys, preferred_element_type=jnp.float32
    )
    grad_keys = jnp.einsum(
        "shqk,sqhd->skhd", grad_scores, query, preferred_element_type=jnp.float32
    )
    return (grad_query, grad_keys, grad_values)


def head_layout():
    columns = lax.axis_size("col")
    per_device = -(-HEADS // columns)
    position = lax.axis_index("col")
    heads_here = position + jnp.arange(per_device, dtype=jnp.int32) * columns
    owner = heads_here // (HEADS // KV_HEADS)
    matches = (owner[:, None] == jnp.arange(KV_HEADS, dtype=jnp.int32)[None, :]) & (
        heads_here[:, None] < HEADS
    )
    return (per_device, per_device * columns, position, matches.astype(jnp.float32))


def pick_heads(selector, table):
    return jnp.einsum(
        "hk,sqkd->sqhd", selector.astype(jnp.bfloat16), table, preferred_element_type=jnp.float32
    ).astype(jnp.bfloat16)


def col_exchange(blocks, gather=False):
    count = lax.axis_size("col")
    shape = blocks.shape if gather else blocks.shape[1:]
    return exchange_call(count, shape, jnp.dtype(blocks.dtype).name, gather)(blocks)


CALLS = {}


def exchange_kernel(count, gather, source, target, own_sem, send_sem, recv_sem):
    me = lax.axis_index("col")
    barrier = pltpu.get_barrier_semaphore()
    for step in range(1, count):
        peer = lax.rem(me + step, count)
        pl.semaphore_signal(
            barrier, inc=1, device_id={"col": peer}, device_id_type=pl.DeviceIdType.MESH
        )
    own = pltpu.make_async_copy(source if gather else source.at[me], target.at[me], own_sem)
    own.start()
    pl.semaphore_wait(barrier, count - 1)
    copies = []
    for step in range(1, count):
        peer = lax.rem(me + step, count)
        copy = pltpu.make_async_remote_copy(
            src_ref=source if gather else source.at[peer],
            dst_ref=target.at[me],
            send_sem=send_sem.at[step],
            recv_sem=recv_sem.at[step],
            device_id={"col": peer},
            device_id_type=pl.DeviceIdType.MESH,
        )
        copy.start()
        copies.append(copy)
    own.wait()
    for copy in copies:
        copy.wait()


def exchange_call(count, shape, dtype, gather):
    key = (count, shape, dtype, gather)
    if key not in CALLS:
        CALLS[key] = pl.pallas_call(
            functools.partial(exchange_kernel, count, gather),
            out_shape=jax.ShapeDtypeStruct((count,) + shape, dtype),
            in_specs=[pl.BlockSpec(memory_space=pltpu.VMEM)],
            out_specs=pl.BlockSpec(memory_space=pltpu.VMEM),
            scratch_shapes=[
                pltpu.SemaphoreType.DMA,
                pltpu.SemaphoreType.DMA((count,)),
                pltpu.SemaphoreType.DMA((count,)),
            ],
            compiler_params=pltpu.CompilerParams(
                collective_id=len(CALLS), has_side_effects=True
            ),
        )
    return CALLS[key]


def col_gather(part):
    blocks = col_exchange(part, gather=True)
    return blocks.transpose(1, 0, 2).reshape(part.shape[0], -1)


def col_scatter(partial_value):
    length, width = partial_value.shape
    count = lax.axis_size("col")
    blocks = partial_value.reshape(length, count, width // count).transpose(1, 0, 2)
    arrived = col_exchange(blocks.astype(jnp.bfloat16))
    return jnp.sum(arrived.astype(jnp.float32), axis=0)


def row_total(values):
    parts = col_exchange(values.reshape(-1, 128), gather=True)
    return jnp.sum(parts, axis=0).reshape(values.shape)


def norm_rows(stream, gain):
    width = stream.shape[1] * lax.axis_size("col")
    squares = row_total(jnp.sum(stream * stream, axis=1))
    scale = lax.rsqrt(squares[:, None] / width + EPS)
    normed = (stream * scale * gain).astype(jnp.bfloat16)
    whole = col_gather(normed)
    return (scale, whole)


def norm_back(grad_normed, stream, scale, gain):
    width = stream.shape[1] * lax.axis_size("col")
    grad_gain = jnp.sum(grad_normed * stream * scale, axis=0)
    scaled = grad_normed * gain
    slope = row_total(jnp.sum(scaled * stream, axis=1))[:, None] / width
    return (scale * scaled - stream * scale**3 * slope, grad_gain)


def feature_back(partial_value):
    return col_scatter(partial_value)


def row_split():
    count = lax.axis_size("row")
    inner = 2 if count % 2 == 0 else 1
    outer = count // inner
    position = lax.axis_index("row")
    return (outer, inner, position // inner, position % inner)


def outer_shift(value, step, outer, inner):
    pairs = []
    for high in range(outer):
        for low in range(inner):
            pairs.append((high * inner + low, ((high + step) % outer) * inner + low))
    return lax.ppermute(value, "row", pairs)


def inner_swap(value, outer):
    pairs = [(at, at ^ 1) for at in range(2 * outer)]
    return lax.ppermute(value, "row", pairs)


def row_gather(shard):
    outer, inner, high, low = row_split()
    held = jnp.zeros((outer,) + shard.shape, shard.dtype)
    held = lax.dynamic_update_slice_in_dim(held, shard[None], high, 0)
    for step in range(1, outer):
        moved = outer_shift(shard, step, outer, inner)
        held = lax.dynamic_update_slice_in_dim(
            held, moved[None], (high + outer - step) % outer, 0
        )
    if inner == 1:
        return held.reshape((outer * shard.shape[0],) + shard.shape[1:])
    other = inner_swap(held, outer)
    first = jnp.where(low == 0, held, other)
    second = jnp.where(low == 0, other, held)
    return jnp.stack([first, second], axis=1).reshape((-1,) + shard.shape[1:])


def row_scatter(grad):
    outer, inner, high, low = row_split()
    width = grad.shape[1]
    blocks = grad.reshape(outer, inner, -1, width)
    if inner == 1:
        sums = blocks[:, 0]
    else:
        first, second = blocks[:, 0], blocks[:, 1]
        leaving = jnp.where(low == 0, second, first).astype(jnp.bfloat16)
        staying = jnp.where(low == 0, first, second)
        sums = staying + inner_swap(leaving, outer).astype(jnp.float32)
    total = lax.dynamic_index_in_dim(sums, high, 0, keepdims=False)
    for step in range(1, outer):
        leaving = lax.dynamic_index_in_dim(sums, (high + step) % outer, 0, keepdims=False)
        total = total + outer_shift(leaving.astype(jnp.bfloat16), step, outer, inner).astype(
            jnp.float32
        )
    return total


def fetch_weights(shards):
    query, key, value, output, gate, up, down = shards
    return (
        row_gather(jnp.concatenate([query, key, value], axis=1)),
        row_gather(output),
        row_gather(jnp.concatenate([gate, up], axis=1)),
        row_gather(down),
    )


def forward_layer(stream, gathered, widths, gain_attn, gain_ffn, cosines, sines):
    joined, output_w, paired, down_w = gathered
    query_cols, key_cols = widths
    length = stream.shape[0]
    sequences = length // SEQ_LEN
    ffn_cols = paired.shape[1] // 2
    columns = lax.axis_size("col")
    per_device, padded, position, selector = head_layout()
    scale_one, normed_one = norm_rows(stream, gain_attn)
    projected = product(normed_one, joined)
    blocks = col_exchange(projected.astype(jnp.bfloat16), gather=True)
    query_all = blocks[:, :, :query_cols].transpose(1, 0, 2).reshape(length, -1)
    key_all = blocks[:, :, query_cols : query_cols + key_cols].transpose(1, 0, 2)
    value_all = blocks[:, :, query_cols + key_cols :].transpose(1, 0, 2)
    query_heads = jnp.pad(
        query_all.reshape(length, HEADS, HEAD_DIM), ((0, 0), (0, padded - HEADS), (0, 0))
    )
    query_heads = query_heads.reshape(length, per_device, columns, HEAD_DIM).transpose(0, 2, 1, 3)
    query_mine = lax.dynamic_index_in_dim(query_heads, position, 1, keepdims=False).reshape(
        sequences, SEQ_LEN, per_device, HEAD_DIM
    )
    query_rot = rotate(query_mine.astype(jnp.float32), cosines, sines).astype(jnp.bfloat16)
    keys_rot = rotate(
        key_all.reshape(sequences, SEQ_LEN, KV_HEADS, HEAD_DIM).astype(jnp.float32), cosines, sines
    ).astype(jnp.bfloat16)
    keys_mine = pick_heads(selector, keys_rot)
    values_mine = pick_heads(selector, value_all.reshape(sequences, SEQ_LEN, KV_HEADS, HEAD_DIM))
    attended, log_total = attend(query_rot, keys_mine, values_mine)
    collected = col_exchange(attended.reshape(length, per_device * HEAD_DIM), gather=True)
    reordered = (
        collected.reshape(columns, length, per_device, HEAD_DIM)
        .transpose(1, 2, 0, 3)
        .reshape(length, padded * HEAD_DIM)
    )
    attended_all = reordered[:, : HEADS * HEAD_DIM]
    middle = stream + product(attended_all, output_w)
    scale_two, normed_two = norm_rows(middle, gain_ffn)
    gate_up = product(normed_two, paired)
    gate = gate_up[:, :ffn_cols]
    up = gate_up[:, ffn_cols:]
    hidden = (jax.nn.silu(gate) * up).astype(jnp.bfloat16)
    hidden_all = col_gather(hidden)
    result = middle + product(hidden_all, down_w)
    saved = (
        scale_one,
        normed_one,
        query_rot,
        keys_mine,
        values_mine,
        log_total,
        attended_all,
        middle,
        scale_two,
        normed_two,
        gate,
        up,
        hidden_all,
    )
    return (result, saved)


def backward_layer(
    stream, gathered, widths, gain_attn, gain_ffn, saved, grad_result, cosines, sines
):
    joined, output_w, paired, down_w = gathered
    query_cols, key_cols = widths
    (
        scale_one,
        normed_one,
        query_rot,
        keys_mine,
        values_mine,
        log_total,
        attended_all,
        middle,
        scale_two,
        normed_two,
        gate,
        up,
        hidden_all,
    ) = saved
    per_device, padded, position, selector = head_layout()
    columns = lax.axis_size("col")
    length = stream.shape[0]
    sequences = length // SEQ_LEN
    ffn_cols = paired.shape[1] // 2
    grad_low = grad_result.astype(jnp.bfloat16)
    grad_down = product(hidden_all.T, grad_low)
    grad_hidden = col_scatter(product(grad_low, down_w.T))
    sigma = jax.nn.sigmoid(gate)
    grad_gate = (grad_hidden * up * sigma * (1.0 + gate * (1.0 - sigma))).astype(jnp.bfloat16)
    grad_up = (grad_hidden * jax.nn.silu(gate)).astype(jnp.bfloat16)
    grad_pair = jnp.concatenate([grad_gate, grad_up], axis=1)
    grad_paired = product(normed_two.T, grad_pair)
    grad_normed_two = feature_back(product(grad_pair, paired.T))
    grad_middle, grad_gain_ffn = norm_back(grad_normed_two, middle, scale_two, gain_ffn)
    grad_middle = grad_middle + grad_result
    middle_low = grad_middle.astype(jnp.bfloat16)
    grad_output_w = product(attended_all.T, middle_low)
    partial_heads = jnp.pad(
        product(middle_low, output_w.T), ((0, 0), (0, (padded - HEADS) * HEAD_DIM))
    )
    partial_heads = partial_heads.reshape(length, per_device, columns, HEAD_DIM).transpose(
        2, 0, 1, 3
    )
    arrived_heads = col_exchange(
        partial_heads.reshape(columns, length, per_device * HEAD_DIM).astype(jnp.bfloat16)
    )
    grad_attended = (
        jnp.sum(arrived_heads.astype(jnp.float32), axis=0)
        .astype(jnp.bfloat16)
        .reshape(sequences, SEQ_LEN, per_device, HEAD_DIM)
    )
    grad_query_rot, grad_keys_mine, grad_values_mine = attend_back(
        query_rot, keys_mine, values_mine, log_total, grad_attended
    )
    grad_query_mine = unrotate(grad_query_rot, cosines, sines).reshape(length, per_device, HEAD_DIM)
    grad_keys_heads = unrotate(grad_keys_mine, cosines, sines).reshape(length, per_device, HEAD_DIM)
    grad_values_heads = grad_values_mine.reshape(length, per_device, HEAD_DIM)
    blank = jnp.zeros((length, columns, per_device, HEAD_DIM), jnp.float32)
    placed = lax.dynamic_update_slice_in_dim(blank, grad_query_mine[:, None], position, 1)
    grad_query_wide = (
        placed.transpose(0, 2, 1, 3)
        .reshape(length, padded, HEAD_DIM)[:, :HEADS]
        .reshape(length, HEADS * HEAD_DIM)
    )
    grad_keys_wide = jnp.einsum(
        "hk,thd->tkd", selector, grad_keys_heads, precision=lax.Precision.HIGHEST
    ).reshape(length, KV_HEADS * HEAD_DIM)
    grad_values_wide = jnp.einsum(
        "hk,thd->tkd", selector, grad_values_heads, precision=lax.Precision.HIGHEST
    ).reshape(length, KV_HEADS * HEAD_DIM)
    outgoing = jnp.concatenate(
        [
            grad_query_wide.reshape(length, columns, query_cols),
            grad_keys_wide.reshape(length, columns, key_cols),
            grad_values_wide.reshape(length, columns, key_cols),
        ],
        axis=2,
    )
    arrived = col_exchange(outgoing.transpose(1, 0, 2).astype(jnp.bfloat16))
    grad_triple = jnp.sum(arrived.astype(jnp.float32), axis=0).astype(jnp.bfloat16)
    grad_joined = product(normed_one.T, grad_triple)
    grad_normed_one = feature_back(product(grad_triple, joined.T))
    grad_stream, grad_gain_attn = norm_back(grad_normed_one, stream, scale_one, gain_attn)
    grad_stream = grad_stream + grad_middle
    row_count = lax.axis_size("row")
    grad_factor = jnp.float32(1.0 / math.sqrt(length * row_count))
    sum_joined = row_scatter(grad_joined) * grad_factor
    sum_paired = row_scatter(grad_paired) * grad_factor
    grads = (
        sum_joined[:, :query_cols],
        sum_joined[:, query_cols : query_cols + key_cols],
        sum_joined[:, query_cols + key_cols :],
        row_scatter(grad_output_w) * grad_factor,
        sum_paired[:, :ffn_cols],
        sum_paired[:, ffn_cols:],
        row_scatter(grad_down) * grad_factor,
        grad_gain_attn * grad_factor,
        grad_gain_ffn * grad_factor,
    )
    return (grad_stream, grads)


def body(
    inputs,
    query_one,
    key_one,
    value_one,
    output_one,
    gate_one,
    up_one,
    down_one,
    attn_gain_one,
    ffn_gain_one,
    query_two,
    key_two,
    value_two,
    output_two,
    gate_two,
    up_two,
    down_two,
    attn_gain_two,
    ffn_gain_two,
    cotangent,
):
    cosines, sines = rope_tables(SEQ_LEN, HEAD_DIM)
    layers = (
        (query_one, key_one, value_one, output_one, gate_one, up_one, down_one),
        (query_two, key_two, value_two, output_two, gate_two, up_two, down_two),
    )
    gains = ((attn_gain_one, ffn_gain_one), (attn_gain_two, ffn_gain_two))
    stream = inputs
    records = []
    widths = (query_one.shape[1], key_one.shape[1])
    fetched = [fetch_weights(layers[level]) for level in range(2)]
    for level in range(2):
        gathered = fetched[level]
        stream_next, saved = forward_layer(
            stream, gathered, widths, gains[level][0], gains[level][1], cosines, sines
        )
        records.append((stream, gathered, saved))
        stream = stream_next
    gradient = cotangent
    reduced = [None, None]
    for level in (1, 0):
        stream_in, gathered, saved = records[level]
        gradient, reduced[level] = backward_layer(
            stream_in,
            gathered,
            widths,
            gains[level][0],
            gains[level][1],
            saved,
            gradient,
            cosines,
            sines,
        )
    gain_sums = lax.psum(
        jnp.stack([reduced[0][7], reduced[0][8], reduced[1][7], reduced[1][8]]), "row"
    )
    first_sums = reduced[0]
    second_sums = reduced[1]
    return (
        stream,
        gradient,
        first_sums[0],
        first_sums[1],
        first_sums[2],
        first_sums[3],
        first_sums[4],
        first_sums[5],
        first_sums[6],
        gain_sums[0],
        gain_sums[1],
        second_sums[0],
        second_sums[1],
        second_sums[2],
        second_sums[3],
        second_sums[4],
        second_sums[5],
        second_sums[6],
        gain_sums[2],
        gain_sums[3],
    )


def solution(mesh):
    return jax.shard_map(
        body,
        mesh=mesh,
        in_specs=(
            P("row", "col"),
            P("row", "col"),
            P("row", "col"),
            P("row", "col"),
            P("row", "col"),
            P("row", "col"),
            P("row", "col"),
            P("row", "col"),
            P("col"),
            P("col"),
            P("row", "col"),
            P("row", "col"),
            P("row", "col"),
            P("row", "col"),
            P("row", "col"),
            P("row", "col"),
            P("row", "col"),
            P("col"),
            P("col"),
            P("row", "col"),
        ),
        out_specs=(
            P("row", "col"),
            P("row", "col"),
            P("row", "col"),
            P("row", "col"),
            P("row", "col"),
            P("row", "col"),
            P("row", "col"),
            P("row", "col"),
            P("row", "col"),
            P("col"),
            P("col"),
            P("row", "col"),
            P("row", "col"),
            P("row", "col"),
            P("row", "col"),
            P("row", "col"),
            P("row", "col"),
            P("row", "col"),
            P("col"),
            P("col"),
        ),
        check_vma=False,
    )
```

```python
import functools
import math

import jax
import jax.numpy as jnp
from jax import lax
from jax.experimental import pallas as pl
from jax.experimental.pallas import tpu as pltpu
from jax.sharding import PartitionSpec as P

HEADS = 15
KV_HEADS = 5
HEAD_DIM = 64
SEQ_LEN = 128


EPS = 1e-05
ROPE_BASE = 100000.0
NEG_FILL = -1e30


def rope_tables(length, depth):
    half = depth // 2
    frequency = ROPE_BASE ** (-(jnp.arange(half, dtype=jnp.float32) * 2.0) / depth)
    angles = jnp.arange(length, dtype=jnp.float32)[:, None] * frequency[None, :]
    return (jnp.cos(angles), jnp.sin(angles))


def rotate(values, cosines, sines):
    half = values.shape[-1] // 2
    first = values[..., :half]
    second = values[..., half:]
    cosine = cosines[:, None, :]
    sine = sines[:, None, :]
    return jnp.concatenate(
        [first * cosine - second * sine, second * cosine + first * sine], axis=-1
    )


def unrotate(values, cosines, sines):
    half = values.shape[-1] // 2
    first = values[..., :half]
    second = values[..., half:]
    cosine = cosines[:, None, :]
    sine = sines[:, None, :]
    return jnp.concatenate(
        [first * cosine + second * sine, second * cosine - first * sine], axis=-1
    )


def product(left, right):
    return jnp.dot(left, right, preferred_element_type=jnp.float32)


def causal_scores(query, keys):
    scale = 1.0 / math.sqrt(query.shape[-1])
    scores = jnp.einsum("sqhd,skhd->shqk", query, keys, preferred_element_type=jnp.float32) * scale
    length = query.shape[1]
    allowed = jnp.arange(length)[None, :] <= jnp.arange(length)[:, None]
    return jnp.where(allowed[None, None], scores, NEG_FILL)


def attend(query, keys, values):
    scores = causal_scores(query, keys)
    top = jnp.max(scores, axis=-1, keepdims=True)
    log_total = top + jnp.log(jnp.sum(jnp.exp(scores - top), axis=-1, keepdims=True))
    shares = jnp.exp(scores - log_total).astype(jnp.bfloat16)
    output = jnp.einsum(
        "shqk,skhd->sqhd", shares, values, preferred_element_type=jnp.float32
    ).astype(jnp.bfloat16)
    return (output, log_total[..., 0])


def attend_back(query, keys, values, log_total, grad_output):
    scale = 1.0 / math.sqrt(query.shape[-1])
    scores = causal_scores(query, keys)
    shares = jnp.exp(scores - log_total[..., None])
    grad_values = jnp.einsum(
        "shqk,sqhd->skhd",
        shares.astype(jnp.bfloat16),
        grad_output,
        preferred_element_type=jnp.float32,
    )
    grad_shares = jnp.einsum(
        "sqhd,skhd->shqk", grad_output, values, preferred_element_type=jnp.float32
    )
    inner = jnp.sum(shares * grad_shares, axis=-1, keepdims=True)
    grad_scores = (shares * (grad_shares - inner) * scale).astype(jnp.bfloat16)
    grad_query = jnp.einsum(
        "shqk,skhd->sqhd", grad_scores, keys, preferred_element_type=jnp.float32
    )
    grad_keys = jnp.einsum(
        "shqk,sqhd->skhd", grad_scores, query, preferred_element_type=jnp.float32
    )
    return (grad_query, grad_keys, grad_values)


def head_layout():
    columns = lax.axis_size("col")
    per_device = -(-HEADS // columns)
    position = lax.axis_index("col")
    heads_here = position + jnp.arange(per_device, dtype=jnp.int32) * columns
    owner = heads_here // (HEADS // KV_HEADS)
    matches = (owner[:, None] == jnp.arange(KV_HEADS, dtype=jnp.int32)[None, :]) & (
        heads_here[:, None] < HEADS
    )
    return (per_device, per_device * columns, position, matches.astype(jnp.float32))


def pick_heads(selector, table):
    return jnp.einsum(
        "hk,sqkd->sqhd", selector.astype(jnp.bfloat16), table, preferred_element_type=jnp.float32
    ).astype(jnp.bfloat16)


def col_exchange(blocks, gather=False):
    count = lax.axis_size("col")
    shape = blocks.shape if gather else blocks.shape[1:]
    return exchange_call(count, shape, jnp.dtype(blocks.dtype).name, gather)(blocks)


CALLS = {}


def exchange_kernel(count, gather, source, target, own_sem, send_sem, recv_sem):
    me = lax.axis_index("col")
    barrier = pltpu.get_barrier_semaphore()
    for step in range(1, count):
        peer = lax.rem(me + step, count)
        pl.semaphore_signal(
            barrier, inc=1, device_id={"col": peer}, device_id_type=pl.DeviceIdType.MESH
        )
    own = pltpu.make_async_copy(source if gather else source.at[me], target.at[me], own_sem)
    own.start()
    pl.semaphore_wait(barrier, count - 1)
    copies = []
    for step in range(1, count):
        peer = lax.rem(me + step, count)
        copy = pltpu.make_async_remote_copy(
            src_ref=source if gather else source.at[peer],
            dst_ref=target.at[me],
            send_sem=send_sem.at[step],
            recv_sem=recv_sem.at[step],
            device_id={"col": peer},
            device_id_type=pl.DeviceIdType.MESH,
        )
        copy.start()
        copies.append(copy)
    own.wait()
    for copy in copies:
        copy.wait()


def gather_kernel(count, source, target, own_sem, send_sem, recv_sem):
    me = lax.axis_index("col")
    half = count // 2
    pair = me + 1 - 2 * lax.rem(me, 2)
    barrier = pltpu.get_barrier_semaphore()
    peers = [pair] + [lax.rem(me + 2 * step, count) for step in range(1, half)]
    for peer in peers:
        pl.semaphore_signal(
            barrier, inc=1, device_id={"col": peer}, device_id_type=pl.DeviceIdType.MESH
        )
    own = pltpu.make_async_copy(source, target.at[me], own_sem)
    own.start()
    pl.semaphore_wait(barrier, half)

    def push(block, slot, at, peer):
        copy = pltpu.make_async_remote_copy(
            src_ref=block,
            dst_ref=target.at[slot],
            send_sem=send_sem.at[at],
            recv_sem=recv_sem.at[at],
            device_id={"col": peer},
            device_id_type=pl.DeviceIdType.MESH,
        )
        copy.start()
        return copy

    crossing = [push(source, me, step, peers[step]) for step in range(1, half)]
    beside = [push(source, me, 0, pair)]
    for step in range(1, half):
        crossing[step - 1].wait_recv()
        slot = lax.rem(me + count - 2 * step, count)
        beside.append(push(target.at[slot], slot, half - 1 + step, pair))
    own.wait()
    for copy in crossing:
        copy.wait_send()
    for copy in beside:
        copy.wait()


def exchange_call(count, shape, dtype, gather):
    key = (count, shape, dtype, gather)
    if key not in CALLS:
        CALLS[key] = pl.pallas_call(
            functools.partial(gather_kernel, count)
            if gather and count % 2 == 0
            else functools.partial(exchange_kernel, count, gather),
            out_shape=jax.ShapeDtypeStruct((count,) + shape, dtype),
            in_specs=[pl.BlockSpec(memory_space=pltpu.VMEM)],
            out_specs=pl.BlockSpec(memory_space=pltpu.VMEM),
            scratch_shapes=[
                pltpu.SemaphoreType.DMA,
                pltpu.SemaphoreType.DMA((count,)),
                pltpu.SemaphoreType.DMA((count,)),
            ],
            compiler_params=pltpu.CompilerParams(
                collective_id=len(CALLS), has_side_effects=True
            ),
        )
    return CALLS[key]


def col_gather(part):
    blocks = col_exchange(part, gather=True)
    return blocks.transpose(1, 0, 2).reshape(part.shape[0], -1)


def col_scatter(partial_value):
    length, width = partial_value.shape
    count = lax.axis_size("col")
    blocks = partial_value.reshape(length, count, width // count).transpose(1, 0, 2)
    arrived = col_exchange(blocks.astype(jnp.bfloat16))
    return jnp.sum(arrived.astype(jnp.float32), axis=0)


def row_total(values):
    parts = col_exchange(values.reshape(-1, 128), gather=True)
    return jnp.sum(parts, axis=0).reshape(values.shape)


def norm_rows(stream, gain):
    width = stream.shape[1] * lax.axis_size("col")
    squares = row_total(jnp.sum(stream * stream, axis=1))
    scale = lax.rsqrt(squares[:, None] / width + EPS)
    normed = (stream * scale * gain).astype(jnp.bfloat16)
    whole = col_gather(normed)
    return (scale, whole)


def norm_back(grad_normed, stream, scale, gain):
    width = stream.shape[1] * lax.axis_size("col")
    grad_gain = jnp.sum(grad_normed * stream * scale, axis=0)
    scaled = grad_normed * gain
    slope = row_total(jnp.sum(scaled * stream, axis=1))[:, None] / width
    return (scale * scaled - stream * scale**3 * slope, grad_gain)


def feature_back(partial_value):
    return col_scatter(partial_value)


def row_split():
    count = lax.axis_size("row")
    inner = 2 if count % 2 == 0 else 1
    outer = count // inner
    position = lax.axis_index("row")
    return (outer, inner, position // inner, position % inner)


def outer_shift(value, step, outer, inner):
    pairs = []
    for high in range(outer):
        for low in range(inner):
            pairs.append((high * inner + low, ((high + step) % outer) * inner + low))
    return lax.ppermute(value, "row", pairs)


def inner_swap(value, outer):
    pairs = [(at, at ^ 1) for at in range(2 * outer)]
    return lax.ppermute(value, "row", pairs)


def row_gather(shard):
    outer, inner, high, low = row_split()
    held = jnp.zeros((outer,) + shard.shape, shard.dtype)
    held = lax.dynamic_update_slice_in_dim(held, shard[None], high, 0)
    for step in range(1, outer):
        moved = outer_shift(shard, step, outer, inner)
        held = lax.dynamic_update_slice_in_dim(
            held, moved[None], (high + outer - step) % outer, 0
        )
    if inner == 1:
        return held.reshape((outer * shard.shape[0],) + shard.shape[1:])
    other = inner_swap(held, outer)
    first = jnp.where(low == 0, held, other)
    second = jnp.where(low == 0, other, held)
    return jnp.stack([first, second], axis=1).reshape((-1,) + shard.shape[1:])


def row_scatter_steps(grad):
    outer, inner, high, low = row_split()
    width = grad.shape[1]
    blocks = grad.reshape(outer, inner, -1, width)
    if inner == 1:
        sums = blocks[:, 0]
    else:
        first, second = blocks[:, 0], blocks[:, 1]
        leaving = jnp.where(low == 0, second, first).astype(jnp.bfloat16)
        staying = jnp.where(low == 0, first, second)
        moved = yield [inner_swap(leaving, outer)]
        sums = staying + moved[0].astype(jnp.float32)
    total = lax.dynamic_index_in_dim(sums, high, 0, keepdims=False)
    moving = []
    for step in range(1, outer):
        leaving = lax.dynamic_index_in_dim(sums, (high + step) % outer, 0, keepdims=False)
        moving.append(outer_shift(leaving.astype(jnp.bfloat16), step, outer, inner))
    arrived = yield moving
    for piece in arrived:
        total = total + piece.astype(jnp.float32)
    yield total


class Reductions:
    def __init__(self):
        self.active = []
        self.totals = {}

    def start(self, name, grad):
        steps = row_scatter_steps(grad)
        self.active.append([name, steps, next(steps)])

    def advance(self, value=None):
        moving = [entry[2] for entry in self.active]
        if value is not None:
            value, moving = lax.optimization_barrier((value, moving))
        remaining = []
        for entry, moved in zip(self.active, moving):
            entry[2] = entry[1].send(moved)
            if isinstance(entry[2], list):
                remaining.append(entry)
            else:
                self.totals[entry[0]] = entry[2]
        self.active = remaining
        return value


def fetch_weights(shards):
    query, key, value, output, gate, up, down = shards
    return (
        row_gather(jnp.concatenate([query, key, value], axis=1)),
        row_gather(output),
        row_gather(jnp.concatenate([gate, up], axis=1)),
        row_gather(down),
    )


def forward_layer(stream, gathered, widths, gain_attn, gain_ffn, cosines, sines):
    joined, output_w, paired, down_w = gathered
    query_cols, key_cols = widths
    length = stream.shape[0]
    sequences = length // SEQ_LEN
    ffn_cols = paired.shape[1] // 2
    columns = lax.axis_size("col")
    per_device, padded, position, selector = head_layout()
    scale_one, normed_one = norm_rows(stream, gain_attn)
    projected = product(normed_one, joined)
    blocks = col_exchange(projected.astype(jnp.bfloat16), gather=True)
    query_all = blocks[:, :, :query_cols].transpose(1, 0, 2).reshape(length, -1)
    key_all = blocks[:, :, query_cols : query_cols + key_cols].transpose(1, 0, 2)
    value_all = blocks[:, :, query_cols + key_cols :].transpose(1, 0, 2)
    query_heads = jnp.pad(
        query_all.reshape(length, HEADS, HEAD_DIM), ((0, 0), (0, padded - HEADS), (0, 0))
    )
    query_heads = query_heads.reshape(length, per_device, columns, HEAD_DIM).transpose(0, 2, 1, 3)
    query_mine = lax.dynamic_index_in_dim(query_heads, position, 1, keepdims=False).reshape(
        sequences, SEQ_LEN, per_device, HEAD_DIM
    )
    query_rot = rotate(query_mine.astype(jnp.float32), cosines, sines).astype(jnp.bfloat16)
    keys_rot = rotate(
        key_all.reshape(sequences, SEQ_LEN, KV_HEADS, HEAD_DIM).astype(jnp.float32), cosines, sines
    ).astype(jnp.bfloat16)
    keys_mine = pick_heads(selector, keys_rot)
    values_mine = pick_heads(selector, value_all.reshape(sequences, SEQ_LEN, KV_HEADS, HEAD_DIM))
    attended, log_total = attend(query_rot, keys_mine, values_mine)
    collected = col_exchange(attended.reshape(length, per_device * HEAD_DIM), gather=True)
    reordered = (
        collected.reshape(columns, length, per_device, HEAD_DIM)
        .transpose(1, 2, 0, 3)
        .reshape(length, padded * HEAD_DIM)
    )
    attended_all = reordered[:, : HEADS * HEAD_DIM]
    middle = stream + product(attended_all, output_w)
    scale_two, normed_two = norm_rows(middle, gain_ffn)
    gate_up = product(normed_two, paired)
    gate = gate_up[:, :ffn_cols]
    up = gate_up[:, ffn_cols:]
    hidden = (jax.nn.silu(gate) * up).astype(jnp.bfloat16)
    hidden_all = col_gather(hidden)
    result = middle + product(hidden_all, down_w)
    saved = (
        scale_one,
        normed_one,
        query_rot,
        keys_mine,
        values_mine,
        log_total,
        attended_all,
        middle,
        scale_two,
        normed_two,
        gate,
        up,
        hidden_all,
    )
    return (result, saved)


def backward_layer(
    stream, gathered, widths, gain_attn, gain_ffn, saved, grad_result, cosines, sines, sums, level
):
    joined, output_w, paired, down_w = gathered
    query_cols, key_cols = widths
    (
        scale_one,
        normed_one,
        query_rot,
        keys_mine,
        values_mine,
        log_total,
        attended_all,
        middle,
        scale_two,
        normed_two,
        gate,
        up,
        hidden_all,
    ) = saved
    per_device, padded, position, selector = head_layout()
    columns = lax.axis_size("col")
    length = stream.shape[0]
    sequences = length // SEQ_LEN
    ffn_cols = paired.shape[1] // 2
    grad_low = grad_result.astype(jnp.bfloat16)
    sums.start(("down", level), product(hidden_all.T, grad_low))
    grad_hidden = col_scatter(product(grad_low, down_w.T))
    sigma = jax.nn.sigmoid(gate)
    grad_gate = (grad_hidden * up * sigma * (1.0 + gate * (1.0 - sigma))).astype(jnp.bfloat16)
    grad_up = (grad_hidden * jax.nn.silu(gate)).astype(jnp.bfloat16)
    grad_pair = jnp.concatenate([grad_gate, grad_up], axis=1)
    grad_normed_two = feature_back(product(grad_pair, paired.T))
    grad_middle, grad_gain_ffn = norm_back(grad_normed_two, middle, scale_two, gain_ffn)
    grad_middle = grad_middle + grad_result
    middle_low = grad_middle.astype(jnp.bfloat16)
    partial_heads = jnp.pad(
        product(middle_low, output_w.T), ((0, 0), (0, (padded - HEADS) * HEAD_DIM))
    )
    partial_heads = partial_heads.reshape(length, per_device, columns, HEAD_DIM).transpose(
        2, 0, 1, 3
    )
    arrived_heads = col_exchange(
        partial_heads.reshape(columns, length, per_device * HEAD_DIM).astype(jnp.bfloat16)
    )
    grad_attended = (
        jnp.sum(arrived_heads.astype(jnp.float32), axis=0)
        .astype(jnp.bfloat16)
        .reshape(sequences, SEQ_LEN, per_device, HEAD_DIM)
    )
    grad_attended = sums.advance(grad_attended)
    sums.start(("paired", level), product(normed_two.T, grad_pair))
    sums.start(("output", level), product(attended_all.T, middle_low))
    grad_query_rot, grad_keys_mine, grad_values_mine = attend_back(
        query_rot, keys_mine, values_mine, log_total, grad_attended
    )
    grad_query_mine = unrotate(grad_query_rot, cosines, sines).reshape(length, per_device, HEAD_DIM)
    grad_keys_heads = unrotate(grad_keys_mine, cosines, sines).reshape(length, per_device, HEAD_DIM)
    grad_values_heads = grad_values_mine.reshape(length, per_device, HEAD_DIM)
    blank = jnp.zeros((length, columns, per_device, HEAD_DIM), jnp.float32)
    placed = lax.dynamic_update_slice_in_dim(blank, grad_query_mine[:, None], position, 1)
    grad_query_wide = (
        placed.transpose(0, 2, 1, 3)
        .reshape(length, padded, HEAD_DIM)[:, :HEADS]
        .reshape(length, HEADS * HEAD_DIM)
    )
    grad_keys_wide = jnp.einsum(
        "hk,thd->tkd", selector, grad_keys_heads, precision=lax.Precision.HIGHEST
    ).reshape(length, KV_HEADS * HEAD_DIM)
    grad_values_wide = jnp.einsum(
        "hk,thd->tkd", selector, grad_values_heads, precision=lax.Precision.HIGHEST
    ).reshape(length, KV_HEADS * HEAD_DIM)
    outgoing = jnp.concatenate(
        [
            grad_query_wide.reshape(length, columns, query_cols),
            grad_keys_wide.reshape(length, columns, key_cols),
            grad_values_wide.reshape(length, columns, key_cols),
        ],
        axis=2,
    )
    arrived = col_exchange(outgoing.transpose(1, 0, 2).astype(jnp.bfloat16))
    grad_triple = jnp.sum(arrived.astype(jnp.float32), axis=0).astype(jnp.bfloat16)
    grad_triple = sums.advance(grad_triple)
    sums.start(("joined", level), product(normed_one.T, grad_triple))
    grad_normed_one = feature_back(product(grad_triple, joined.T))
    grad_stream, grad_gain_attn = norm_back(grad_normed_one, stream, scale_one, gain_attn)
    grad_stream = grad_stream + grad_middle
    return (grad_stream, (grad_gain_attn, grad_gain_ffn))


def body(
    inputs,
    query_one,
    key_one,
    value_one,
    output_one,
    gate_one,
    up_one,
    down_one,
    attn_gain_one,
    ffn_gain_one,
    query_two,
    key_two,
    value_two,
    output_two,
    gate_two,
    up_two,
    down_two,
    attn_gain_two,
    ffn_gain_two,
    cotangent,
):
    cosines, sines = rope_tables(SEQ_LEN, HEAD_DIM)
    layers = (
        (query_one, key_one, value_one, output_one, gate_one, up_one, down_one),
        (query_two, key_two, value_two, output_two, gate_two, up_two, down_two),
    )
    gains = ((attn_gain_one, ffn_gain_one), (attn_gain_two, ffn_gain_two))
    stream = inputs
    records = []
    widths = (query_one.shape[1], key_one.shape[1])
    fetched = [fetch_weights(layers[level]) for level in range(2)]
    for level in range(2):
        gathered = fetched[level]
        stream_next, saved = forward_layer(
            stream, gathered, widths, gains[level][0], gains[level][1], cosines, sines
        )
        records.append((stream, gathered, saved))
        stream = stream_next
    gradient = cotangent
    sums = Reductions()
    gain_grads = {}
    for level in (1, 0):
        stream_in, gathered, saved = records[level]
        gradient, gain_grads[level] = backward_layer(
            stream_in,
            gathered,
            widths,
            gains[level][0],
            gains[level][1],
            saved,
            gradient,
            cosines,
            sines,
            sums,
            level,
        )
        gradient = sums.advance(gradient)
    gain_sums = lax.psum(jnp.stack(gain_grads[0] + gain_grads[1]), "row")
    while sums.active:
        gain_sums = sums.advance(gain_sums)
    grad_factor = jnp.float32(1.0 / math.sqrt(inputs.shape[0] * lax.axis_size("row")))
    gain_sums = gain_sums * grad_factor
    query_cols, key_cols = widths
    ffn_cols = gate_one.shape[1]
    reduced = []
    for level in range(2):
        joined = sums.totals["joined", level] * grad_factor
        paired = sums.totals["paired", level] * grad_factor
        reduced.append(
            (
                joined[:, :query_cols],
                joined[:, query_cols : query_cols + key_cols],
                joined[:, query_cols + key_cols :],
                sums.totals["output", level] * grad_factor,
                paired[:, :ffn_cols],
                paired[:, ffn_cols:],
                sums.totals["down", level] * grad_factor,
            )
        )
    first_sums = reduced[0]
    second_sums = reduced[1]
    return (
        stream,
        gradient,
        first_sums[0],
        first_sums[1],
        first_sums[2],
        first_sums[3],
        first_sums[4],
        first_sums[5],
        first_sums[6],
        gain_sums[0],
        gain_sums[1],
        second_sums[0],
        second_sums[1],
        second_sums[2],
        second_sums[3],
        second_sums[4],
        second_sums[5],
        second_sums[6],
        gain_sums[2],
        gain_sums[3],
    )


def solution(mesh):
    return jax.shard_map(
        body,
        mesh=mesh,
        in_specs=(
            P("row", "col"),
            P("row", "col"),
            P("row", "col"),
            P("row", "col"),
            P("row", "col"),
            P("row", "col"),
            P("row", "col"),
            P("row", "col"),
            P("col"),
            P("col"),
            P("row", "col"),
            P("row", "col"),
            P("row", "col"),
            P("row", "col"),
            P("row", "col"),
            P("row", "col"),
            P("row", "col"),
            P("col"),
            P("col"),
            P("row", "col"),
        ),
        out_specs=(
            P("row", "col"),
            P("row", "col"),
            P("row", "col"),
            P("row", "col"),
            P("row", "col"),
            P("row", "col"),
            P("row", "col"),
            P("row", "col"),
            P("row", "col"),
            P("col"),
            P("col"),
            P("row", "col"),
            P("row", "col"),
            P("row", "col"),
            P("row", "col"),
            P("row", "col"),
            P("row", "col"),
            P("row", "col"),
            P("col"),
            P("col"),
        ),
        check_vma=False,
    )
```
